32 devices in a mesh: store: 8 (over z, y), tensor: 4 (over x, core).
Axes of the slice: x: 2, y: 2, z: 4, core: 2. Of those that a mesh axis runs over, the one named last changes fastest.
Arguments:
- tokens: bfloat16 [8192, 8192], P('store', 'tensor'), may hold values from -1200 to 1200
- norm_gain: float32 [8192], P('tensor'), may hold values from 0.1 to 1.9
- kv_weight: bfloat16 [8192, 2, 1024], P('tensor'), may hold values from -0.0625 to 0.0625
- adapter_down: bfloat16 [32, 8192, 128], P('store', 'tensor'), may hold values from -0.0625 to 0.0625
- adapter_up: bfloat16 [32, 2, 64, 1024], P('store', None, None, 'tensor'), may hold values from -0.75 to 0.75
- token_adapters: int32 [8192, 1], P('store'), may hold values from 0 to 31; in each aligned block of 1024 rows (0 to 1023, 1024 to 2047, ...) at most 40 rows name the same one
- adapter_slot: int32 [32], replicated, may hold values from 0 to 31, each once
- request_lengths: int32 [16], replicated, may hold values from 1 to 4096, 8192 in all
Outputs:
- new_keys: bfloat16 [8192, 1024], P('store', 'tensor')
- new_values: bfloat16 [8192, 1024], P('store', 'tensor')
The draws below stay inside these ranges and needn't reach their ends.
Inputs may be any that keep to these rules, and one draw needn't show every extreme that they name: `token_adapters`: among the 1024 tokens of one index of store no adapter is named more than 40 times; in every draw some adapter is named exactly 40 times by the tokens of some index. `adapter_slot`: each row 0 to 31 appears once. `request_lengths`: the lengths sum to 8192; the largest is exactly 4096.
All inputs are finite; a program needn't handle non-finite values.
Results may differ from the reference program's by a relative error of at most 0.0061.
Values may be sent and summed in bfloat16 or wider, within the bound.
A program may use at most 128 MiB of HBM per device.

```python
import math
import jax
import jax.numpy as jnp
import numpy as np
from jax import lax

D = 8192
KV = 1024
HEAD = 128
ADAPTER_RANK = 64
TOK_DEV = 1024
ADAPTER_COUNT = 32
TOKENS = 8192
TOKENS_PER_ADAPT = 40
REQS = 16
REQ_MOST = 4096
N_STORE = 8


def draw_tokens(key, part):
    column_key = jax.random.fold_in(key, 11)
    row_key = jax.random.fold_in(key, 23)
    value_key = jax.random.fold_in(key, 37)
    columns = jnp.arange(D, dtype=jnp.float32)
    column_scale = jnp.exp(math.log(3.0) * columns / (D - 1) + math.log(10.0) * jax.random.uniform(column_key, (D,), jnp.float32))
    row_scale = jnp.exp(math.log(10.0) * jax.random.uniform(row_key, (TOKENS, 1), jnp.float32))
    values = jax.random.truncated_normal(value_key, -4.0, 4.0, (TOKENS, D), jnp.float32)
    return (values * column_scale[None, :] * row_scale).astype(jnp.bfloat16)


def levels(own_key, shape, shards, smallest, high):
    gain, own = 1.0, jax.random.fold_in(own_key, 6)
    for position, blocks in shards:
        heights = jnp.exp(jax.random.uniform(jax.random.fold_in(own, position), (blocks,), jnp.float32, smallest / len(shards), high / len(shards)))
        gain = gain * jnp.repeat(heights, shape[position] // blocks).reshape([-1 if axis == position else 1 for axis in range(len(shape))])
    return gain


def split_up(number_of, total, limit, lean):
    portions = [(1 << 20) // math.isqrt(rank ** lean) + 1 for rank in range(2, number_of + 1)]
    surplus, holding = total - limit - (number_of - 1), [1] * (number_of - 1)
    while surplus > 0:
        free = [i for i in range(number_of - 1) if holding[i] < limit]
        pool, remaining = sum([portions[i] for i in free]), surplus
        for i in free:
            extra = min(limit - holding[i], max(1, remaining * portions[i] // pool), surplus)
            holding[i] = holding[i] + extra
            surplus = surplus - extra
    return np.array([limit] + holding)


def ragged_sizes(own_key, count, total, limit, slope):
    if count == 2:
        one = jax.random.randint(own_key, (), max(1, total - limit), min(limit, total - 1) + 1)
        return jnp.stack([one, total - one])
    sizes = jnp.asarray(split_up(count, total, limit, slope), jnp.int32)
    twos = (count - 1) // 2
    giver, receiver = sizes[1:1 + 2 * twos:2], sizes[2:2 + 2 * twos:2]
    slack = jnp.minimum(giver - 1, limit - receiver)
    passed = jax.random.randint(jax.random.fold_in(own_key, 1), (twos,), 0, 1 << 20) % (slack + 1)
    sizes = sizes.at[1:1 + 2 * twos:2].set(giver - passed).at[2:2 + 2 * twos:2].set(receiver + passed)
    return sizes[jax.random.permutation(jax.random.fold_in(own_key, 2), count)]


def assign_block(own_key, own, number, rows, number_of, top, limit, slope):
    sequence = jax.random.permutation(own_key, number_of)
    heavy_load, usual = load_shares(number_of, rows * top, limit, slope, True), load_shares(number_of, rows * top, limit, slope, False)
    places = jnp.arange(number_of)

    def named(sizes, turn):
        used = int((sizes > 0).sum())
        fixed = max(1, used // 4)
        moved = fixed + (places - fixed + turn * (used - fixed)) % max(1, number_of - fixed)
        return jnp.zeros((number_of,), jnp.int32).at[sequence[jnp.where(places < fixed, places, moved)]].set(jnp.asarray(sizes, jnp.int32))

    sizes = jnp.where(number % 4 == 0, named(heavy_load, number // 4), named(usual, number - number // 4 - 1))
    mixed = jax.random.permutation(jax.random.fold_in(own, 3), number_of)
    donor, sink = mixed[0:number_of // 2 * 2:2], mixed[1:number_of // 2 * 2:2]
    margin = jnp.minimum(sizes[donor] - 1, limit - sizes[sink]) // 2
    margin = jnp.where((donor == sequence[0]) | (sink == sequence[0]) | (sizes[sink] == 0), 0, jnp.maximum(margin, 0))
    moved = jax.random.randint(jax.random.fold_in(own, 4), (number_of // 2,), 0, 1 << 20) % (margin + 1)
    sizes = sizes.at[donor].add(-moved).at[sink].add(moved)
    members = jnp.searchsorted(jnp.cumsum(sizes), jnp.arange(rows * top), side="right").astype(jnp.int32)
    table = members.reshape(top, rows).T
    table = table[jax.random.permutation(jax.random.fold_in(own, 1), rows)]
    turn = jax.random.randint(jax.random.fold_in(own, 2), (rows, 1), 0, top)
    return jnp.take_along_axis(table, (jnp.arange(top)[None, :] + turn) % top, axis=1)


def load_shares(number_of, total, reach, lean, full):
    portions = [(1 << 20) // math.isqrt(rank ** lean) + 1 for rank in range(1, number_of + 1)]
    largest = reach if full else min(reach, max(-(-total // number_of), total * portions[0] // sum(portions)))
    least = 1 if total - largest >= number_of - 1 else 0
    counts, surplus = [largest] + [least] * (number_of - 1), total - largest - least * (number_of - 1)
    while surplus > 0:
        candidates = [i for i in range(1, number_of) if counts[i] < largest] or [i for i in range(1, number_of) if counts[i] < reach]
        pool, left = sum([portions[i] for i in candidates]), surplus
        for i in candidates:
            more = min(reach - counts[i], max(1, left * portions[i] // pool), surplus)
            counts[i] = counts[i] + more
            surplus = surplus - more
    return np.array(counts)


def centred(rng, extent, spread, most, pieces=(), kind=jnp.bfloat16):
    drawn = jax.random.normal(rng, extent, jnp.float32) * spread
    if len(pieces) > 0:
        drawn = levels(rng, extent, pieces, -0.22, 0.18) * drawn
    return jnp.clip(drawn, min=-most, max=most).astype(kind)


def setup_inputs(seed: int = 0) -> dict:
    key_of = jax.random.split(jax.random.key(seed), 9)
    tokens = draw_tokens(jax.random.fold_in(key_of[8], 71), 0)
    norm_gain = jnp.clip(1.0 + 0.18 * jax.random.normal(key_of[1], (D,), jnp.float32), 0.1, 1.9)
    kv_weight = centred(key_of[2], (D, 2, KV), D ** -0.5, 0.0625, ((0, 4),))
    adapter_down = centred(key_of[3], (ADAPTER_COUNT, D, 2 * ADAPTER_RANK), D ** -0.5, 0.0625, ((0, 8), (1, 4)))
    adapter_up = centred(key_of[4], (ADAPTER_COUNT, 2, ADAPTER_RANK, KV), ADAPTER_RANK ** -0.5, 0.75, ((0, 8), (3, 4)))
    token_adapters_keys = jax.random.split(jax.random.fold_in(key_of[5], 1), TOKENS // TOK_DEV)
    token_adapters_turns = jax.random.permutation(jax.random.fold_in(key_of[5], 3), TOKENS // TOK_DEV)
    token_adapters = jax.vmap(lambda own, number: assign_block(jax.random.fold_in(key_of[5], 2), own, number, TOK_DEV, ADAPTER_COUNT, 1, TOKENS_PER_ADAPT, 2))(token_adapters_keys, token_adapters_turns).reshape((TOKENS, 1))
    adapter_slot = jax.random.permutation(key_of[6], ADAPTER_COUNT).astype(jnp.int32)
    request_lengths = ragged_sizes(key_of[7], REQS, TOKENS, REQ_MOST, 2).astype(jnp.int32)
    return dict(tokens=tokens, norm_gain=norm_gain, kv_weight=kv_weight, adapter_down=adapter_down, adapter_up=adapter_up, token_adapters=token_adapters, adapter_slot=adapter_slot, request_lengths=request_lengths)


epsilon = 1e-05
adapter_scale = 2.0
rope_theta = 500000.0

def place_rows(adapter_ids, adapter_slot, capacity):
    catalog = jnp.arange(adapter_slot.shape[0], dtype=jnp.int32)
    slot_rows = lax.optimization_barrier(jnp.sum(jnp.where(adapter_ids[:, None] == catalog[None, :], adapter_slot[None, :], 0), axis=1)).astype(jnp.int32)
    row_order = jnp.arange(adapter_ids.shape[0], dtype=jnp.int32)
    same_earlier = (adapter_ids[:, None] == adapter_ids[None, :]) & (row_order[None, :] < row_order[:, None])
    rank_rows = lax.optimization_barrier(jnp.sum(same_earlier.astype(jnp.int32), axis=1)).astype(jnp.int32)
    return (slot_rows * capacity + rank_rows).astype(jnp.int32)

def positions_of(first_row, row_count, lengths):
    global_rows = first_row + jnp.arange(row_count, dtype=jnp.int32)
    request_ends = jnp.cumsum(lengths).astype(jnp.int32)
    preceding = lax.optimization_barrier(jnp.sum(jnp.where(request_ends[None, :] <= global_rows[:, None], lengths[None, :], 0), axis=1)).astype(jnp.int32)
    return (global_rows - preceding).astype(jnp.int32)

def rotate(states, positions):
    per_head = states.reshape(states.shape[0], -1, HEAD)
    half_size = HEAD // 2
    frequency = jnp.exp(jnp.arange(half_size, dtype=jnp.float32) * (-2.0 * math.log(rope_theta) / HEAD))
    angles = positions.astype(jnp.float32)[:, None] * frequency[None, :]
    cos_part = jnp.concatenate([jnp.cos(angles), jnp.cos(angles)], axis=1)[:, None, :]
    sin_part = jnp.concatenate([jnp.sin(angles), jnp.sin(angles)], axis=1)[:, None, :]
    low_half = per_head[..., :half_size]
    high_half = per_head[..., half_size:]
    turned = jnp.concatenate([-high_half, low_half], axis=-1)
    return (per_head * cos_part + turned * sin_part).reshape(states.shape)

def reference(tokens, norm_gain, kv_weight, adapter_down, adapter_up, token_adapters, adapter_slot, request_lengths):
    widened = tokens.astype(jnp.float32)
    squares = lax.optimization_barrier(jnp.sum(widened * widened, axis=1))
    normed = (widened * lax.rsqrt(squares / D + epsilon)[:, None] * norm_gain[None, :]).astype(jnp.bfloat16)
    base_part = jnp.dot(normed, kv_weight.reshape(D, 2 * KV), preferred_element_type=jnp.float32).reshape(TOKENS, 2, KV)
    down_float = adapter_down.astype(jnp.float32)
    up_float = adapter_up.astype(jnp.float32)

    def block_delta(block_args):
        block_rows, block_ids = block_args
        targets = place_rows(block_ids, adapter_slot, TOKENS_PER_ADAPT)
        buffer = jnp.zeros((ADAPTER_COUNT * TOKENS_PER_ADAPT, D), jnp.bfloat16).at[targets].set(block_rows)
        buffer = buffer.reshape(ADAPTER_COUNT, TOKENS_PER_ADAPT, D)
        down_projected = jnp.einsum('acd,adr->acr', buffer.astype(jnp.float32), down_float)
        rank_activation = (down_projected * adapter_scale).astype(jnp.bfloat16).reshape(ADAPTER_COUNT, TOKENS_PER_ADAPT, 2, ADAPTER_RANK)
        update_rows = jnp.einsum('acjr,ajrk->acjk', rank_activation.astype(jnp.float32), up_float).astype(jnp.bfloat16)
        return update_rows.reshape(ADAPTER_COUNT * TOKENS_PER_ADAPT, 2, KV)[targets]
    delta_rows = lax.map(block_delta, (normed.reshape(N_STORE, TOK_DEV, D), token_adapters[:, 0].reshape(N_STORE, TOK_DEV)))
    delta_rows = delta_rows.reshape(TOKENS, 2, KV)
    combined = base_part + delta_rows.astype(jnp.float32)
    positions = positions_of(jnp.zeros((), jnp.int32), TOKENS, request_lengths)
    new_keys = rotate(combined[:, 0, :], positions).astype(jnp.bfloat16)
    new_values = combined[:, 1, :].astype(jnp.bfloat16)
    return (new_keys, new_values)
```

```python
import math

import jax
import jax.numpy as jnp
from jax import lax
from jax.sharding import PartitionSpec as P

D = 8192
HEAD = 128
ADAPTER_RANK = 64


epsilon = 1e-05
adapter_scale = 2.0
rope_theta = 500000.0


def place_rows(adapter_ids, adapter_slot, capacity):
    catalog = jnp.arange(adapter_slot.shape[0], dtype=jnp.int32)
    slot_rows = jnp.sum(
        jnp.where(adapter_ids[:, None] == catalog[None, :], adapter_slot[None, :], 0), axis=1
    )
    row_order = jnp.arange(adapter_ids.shape[0], dtype=jnp.int32)
    same_earlier = (adapter_ids[:, None] == adapter_ids[None, :]) & (
        row_order[None, :] < row_order[:, None]
    )
    rank_rows = jnp.sum(same_earlier.astype(jnp.int32), axis=1)
    return slot_rows * capacity + rank_rows


def positions_of(first_row, row_count, lengths):
    global_rows = first_row + jnp.arange(row_count, dtype=jnp.int32)
    request_ends = jnp.cumsum(lengths)
    preceding = jnp.sum(
        jnp.where(request_ends[None, :] <= global_rows[:, None], lengths[None, :], 0), axis=1
    )
    return global_rows - preceding


def rotate(states, positions):
    per_head = states.reshape(states.shape[0], -1, HEAD)
    half_size = HEAD // 2
    frequency = jnp.exp(
        jnp.arange(half_size, dtype=jnp.float32) * (-2.0 * math.log(rope_theta) / HEAD)
    )
    angles = positions.astype(jnp.float32)[:, None] * frequency[None, :]
    cos_part = jnp.concatenate([jnp.cos(angles), jnp.cos(angles)], axis=1)[:, None, :]
    sin_part = jnp.concatenate([jnp.sin(angles), jnp.sin(angles)], axis=1)[:, None, :]
    low_half = per_head[..., :half_size]
    high_half = per_head[..., half_size:]
    turned = jnp.concatenate([-high_half, low_half], axis=-1)
    return (per_head * cos_part + turned * sin_part).reshape(states.shape)


def xor_pairs(size, step):
    return [(index, index ^ step) for index in range(size)]


def local(
    tokens,
    norm_gain,
    kv_weight,
    adapter_down,
    adapter_up,
    token_adapters,
    adapter_slot,
    request_lengths,
):
    row_count = tokens.shape[0]
    adapter_total = adapter_slot.shape[0]
    capacity = max(2, 5 * row_count // (4 * adapter_total))
    store_size = lax.axis_size("store")
    per_owner = adapter_down.shape[0]
    kv_local = adapter_up.shape[3]
    me = lax.axis_index("store")
    block = per_owner * capacity
    permuted = store_size <= 8
    widened = tokens.astype(jnp.float32)
    squares = lax.psum(jnp.sum(widened * widened, axis=1), "tensor")
    normed = (widened * lax.rsqrt(squares / D + epsilon)[:, None] * norm_gain[None, :]).astype(
        jnp.bfloat16
    )
    targets = place_rows(token_adapters[:, 0], adapter_slot, capacity)
    if permuted:
        targets = ((targets // block) ^ me) * block + targets % block
    places = jnp.arange(adapter_total * capacity, dtype=jnp.int32)
    choose = (places[:, None] == targets[None, :]).astype(jnp.bfloat16)
    partial_value = jnp.einsum("td,djk->tjk", normed, kv_weight, preferred_element_type=jnp.float32)
    partial_value, adapter_down = lax.optimization_barrier((partial_value, adapter_down))
    base_part = lax.psum_scatter(partial_value, "tensor", scatter_dimension=2, tiled=True)

    def project(rows):
        return jnp.einsum(
            "lcd,ldr->lcr",
            rows.reshape(per_owner, -1, rows.shape[-1]),
            adapter_down,
            preferred_element_type=jnp.float32,
        )

    def raise_rows(total):
        middle = (total * adapter_scale).astype(jnp.bfloat16)
        split_rank = middle.reshape(middle.shape[:3] + (2, ADAPTER_RANK))
        rows = jnp.einsum(
            "slcjr,ljrk->slcjk", split_rank, adapter_up, preferred_element_type=jnp.float32
        )
        return rows.astype(jnp.bfloat16).reshape(middle.shape[0], block, 2 * kv_local)

    if permuted:
        order = [4, 5, 6, 7, 1, 2, 3] if store_size == 8 else list(range(1, store_size))
        arrived = {}
        for step in order:
            part = jnp.dot(
                choose[step * block : (step + 1) * block], normed,
                preferred_element_type=jnp.float32,
            ).astype(jnp.bfloat16)
            arrived[step] = lax.ppermute(part, "store", xor_pairs(store_size, step))
        arrived[0] = jnp.dot(
            choose[:block], normed, preferred_element_type=jnp.float32
        ).astype(jnp.bfloat16)
        back = {}
        half = max(1, store_size // 2)
        for group in (list(range(half)), list(range(half, store_size))):
            total = lax.psum(jnp.stack([project(arrived[step]) for step in group]), "tensor")
            raised = raise_rows(total)
            for place, step in enumerate(group):
                back[step] = raised[place]
                if step:
                    back[step] = lax.ppermute(back[step], "store", xor_pairs(store_size, step))
        returned = jnp.concatenate([back[step] for step in range(store_size)], axis=0)
    else:
        send_rows = jnp.dot(choose, normed, preferred_element_type=jnp.float32).astype(jnp.bfloat16)
        send_rows = send_rows.reshape(store_size, per_owner, capacity, -1)
        arrived = lax.all_to_all(send_rows, "store", split_axis=0, concat_axis=0, tiled=True)
        down_projected = jnp.einsum(
            "slcd,ldr->slcr", arrived, adapter_down, preferred_element_type=jnp.float32
        )
        raised = raise_rows(lax.psum(down_projected, "tensor"))
        returned = lax.all_to_all(raised, "store", split_axis=0, concat_axis=0, tiled=True)
        returned = returned.reshape(-1, 2 * kv_local)
    delta_rows = lax.dot_general(
        choose, returned, (((0,), (0,)), ((), ())), preferred_element_type=jnp.float32
    ).reshape(row_count, 2, kv_local)
    combined = base_part + delta_rows
    positions = positions_of(lax.axis_index("store") * row_count, row_count, request_lengths)
    new_keys = rotate(combined[:, 0, :], positions).astype(jnp.bfloat16)
    new_values = combined[:, 1, :].astype(jnp.bfloat16)
    return (new_keys, new_values)


def solution(mesh):
    return jax.shard_map(
        local,
        mesh=mesh,
        in_specs=(
            P("store", "tensor"),
            P("tensor"),
            P("tensor", None, None),
            P("store", "tensor", None),
            P("store", None, None, "tensor"),
            P("store", None),
            P(),
            P(),
        ),
        out_specs=(P("store", "tensor"), P("store", "tensor")),
        check_vma=False,
    )
```

```python
import functools
import math

import jax
import jax.numpy as jnp
from jax import lax
from jax.experimental import pallas as pl
from jax.experimental.pallas import tpu as pltpu
from jax.sharding import PartitionSpec as P

D = 8192
HEAD = 128
ADAPTER_RANK = 64


epsilon = 1e-05
adapter_scale = 2.0
rope_theta = 500000.0


def place_rows(adapter_ids, adapter_slot, capacity):
    catalog = jnp.arange(adapter_slot.shape[0], dtype=jnp.int32)
    slot_rows = jnp.sum(
        jnp.where(adapter_ids[:, None] == catalog[None, :], adapter_slot[None, :], 0), axis=1
    )
    row_order = jnp.arange(adapter_ids.shape[0], dtype=jnp.int32)
    same_earlier = (adapter_ids[:, None] == adapter_ids[None, :]) & (
        row_order[None, :] < row_order[:, None]
    )
    rank_rows = jnp.sum(same_earlier.astype(jnp.int32), axis=1)
    return slot_rows * capacity + rank_rows


def positions_of(first_row, row_count, lengths):
    global_rows = first_row + jnp.arange(row_count, dtype=jnp.int32)
    request_ends = jnp.cumsum(lengths)
    preceding = jnp.sum(
        jnp.where(request_ends[None, :] <= global_rows[:, None], lengths[None, :], 0), axis=1
    )
    return global_rows - preceding


def rotate(states, positions):
    per_head = states.reshape(states.shape[0], -1, HEAD)
    half_size = HEAD // 2
    frequency = jnp.exp(
        jnp.arange(half_size, dtype=jnp.float32) * (-2.0 * math.log(rope_theta) / HEAD)
    )
    angles = positions.astype(jnp.float32)[:, None] * frequency[None, :]
    cos_part = jnp.concatenate([jnp.cos(angles), jnp.cos(angles)], axis=1)[:, None, :]
    sin_part = jnp.concatenate([jnp.sin(angles), jnp.sin(angles)], axis=1)[:, None, :]
    low_half = per_head[..., :half_size]
    high_half = per_head[..., half_size:]
    turned = jnp.concatenate([-high_half, low_half], axis=-1)
    return (per_head * cos_part + turned * sin_part).reshape(states.shape)


MESH = pl.DeviceIdType.MESH


def send_order(size):
    return sorted(range(1, size), key=lambda step: (abs(2 * step - size), step))


def fused_kernel(
    stores,
    tensors,
    tok,
    gain,
    trow,
    tcol,
    cos_t,
    sin_t,
    up,
    w_hbm,
    down_hbm,
    keys_o,
    vals_o,
    g,
    w,
    down,
    sq_out,
    sq_in,
    snd,
    rcv,
    acc,
    base_out,
    base_in,
    low_out,
    low_in,
    ret_out,
    ret_in,
    load_sem,
    sq_ss,
    sq_rs,
    tok_ss,
    tok_rs,
    base_ss,
    base_rs,
    low_ss,
    low_rs,
    ret_ss,
    ret_rs,
):
    rows, width = tok.shape
    per_owner = down.shape[0]
    block = rcv.shape[1]
    capacity = block // per_owner
    kv_local = up.shape[3]
    kv_whole = kv_local * tensors
    me_s = lax.axis_index("store")
    me_t = lax.axis_index("tensor")

    load_w = pltpu.make_async_copy(w_hbm, w, load_sem.at[0])
    load_d = pltpu.make_async_copy(down_hbm, down, load_sem.at[1])
    load_w.start()
    load_d.start()

    barrier = pltpu.get_barrier_semaphore()
    for step in range(1, stores):
        pl.semaphore_signal(
            barrier, inc=1, device_id={"store": (me_s + step) % stores}, device_id_type=MESH
        )
    for step in range(1, tensors):
        pl.semaphore_signal(
            barrier, inc=1, device_id={"tensor": (me_t + step) % tensors}, device_id_type=MESH
        )
    pl.semaphore_wait(barrier, stores + tensors - 2)

    def remote(src, dst, ss, rs, axis, target):
        return pltpu.make_async_remote_copy(
            src_ref=src, dst_ref=dst, send_sem=ss, recv_sem=rs,
            device_id={axis: target}, device_id_type=MESH,
        )

    def to_tensor(step):
        return (me_t + step) % tensors

    tile = 128

    def scale(i, _):
        at = pl.ds(pl.multiple_of(i * tile, tile), tile)
        x = tok[at, :].astype(jnp.float32)
        g[at, :] = (x * gain[...]).astype(jnp.bfloat16)
        total = x[:, 0:128] * x[:, 0:128]
        for lane in range(1, width // 128):
            part = x[:, lane * 128 : (lane + 1) * 128]
            total = total + part * part
        sq_out[at, :] = total
        return 0

    lax.fori_loop(0, rows // tile, scale, 0)

    sq_copies = [
        remote(sq_out, sq_in.at[m - 1], sq_ss.at[m - 1], sq_rs.at[m - 1], "tensor", to_tensor(m))
        for m in range(1, tensors)
    ]

    chunk = 512
    order = send_order(stores)
    tok_copies = {
        step: remote(
            snd.at[step - 1], rcv.at[step], tok_ss.at[step], tok_rs.at[step],
            "store", (me_s + step) % stores,
        )
        for step in order
    }

    def pick(step, dst):
        places = lax.broadcasted_iota(jnp.int32, (block, rows), 0) + step * block
        choose = jnp.where(places == trow[...], 1.0, 0.0).astype(jnp.bfloat16)

        def part(i, _):
            at = pl.ds(pl.multiple_of(i * chunk, chunk), chunk)
            dst[:, at] = jnp.dot(
                choose, g[:, at], preferred_element_type=jnp.float32
            ).astype(jnp.bfloat16)
            return 0

        lax.fori_loop(0, width // chunk, part, 0)

    for place, step in enumerate(order):
        pick(step, snd.at[step - 1])
        if place:
            tok_copies[order[place - 1]].start()
    pick(0, rcv.at[0])
    tok_copies[order[-1]].start()
    for copy in sq_copies:
        copy.start()

    load_w.wait()
    base_copies = [
        remote(
            base_out.at[m - 1], base_in.at[m - 1], base_ss.at[m - 1], base_rs.at[m - 1],
            "tensor", to_tensor(m),
        )
        for m in range(1, tensors)
    ]
    mt = 256
    for m in list(range(1, tensors)) + [0]:
        for j in range(2):
            cols = pl.ds(
                pl.multiple_of(j * kv_whole + to_tensor(m) * kv_local, kv_local), kv_local
            )

            def base(i, _, m=m, j=j, cols=cols):
                at = pl.ds(pl.multiple_of(i * mt, mt), mt)
                r = jnp.dot(g[at, :], w[:, cols], preferred_element_type=jnp.float32)
                if m:
                    base_out[m - 1, at, j * kv_local : (j + 1) * kv_local] = r.astype(jnp.bfloat16)
                else:
                    acc[at, j * kv_local : (j + 1) * kv_local] = r
                return 0

            lax.fori_loop(0, rows // mt, base, 0)
        if m > 1:
            base_copies[m - 2].start()
        if m == 0:
            base_copies[tensors - 2].start()

    load_d.wait()
    owner_of = lax.broadcasted_iota(jnp.int32, (block, 1), 0) // capacity
    low_copies = {}

    def lower(step):
        if step:
            tok_copies[step].wait_recv()
        x = rcv[step]
        low = jnp.zeros((block, 128), jnp.float32)
        for l in range(per_owner):
            r = jnp.dot(x, down[l], preferred_element_type=jnp.float32)
            low = jnp.where(owner_of == l, r, low)
        low_out[step] = low
        for m in range(1, tensors):
            low_copies[step, m] = remote(
                low_out.at[step], low_in.at[m - 1, step], low_ss.at[step, m - 1],
                low_rs.at[step, m - 1], "tensor", to_tensor(m),
            )
            low_copies[step, m].start()

    ret_copies = {}

    def raise_back(step):
        total = low_out[step]
        for m in range(1, tensors):
            low_copies[step, m].wait_recv()
            total = total + low_in[m - 1, step]
        middle = (total * adapter_scale).astype(jnp.bfloat16)
        for j in range(2):
            mj = middle[:, j * ADAPTER_RANK : (j + 1) * ADAPTER_RANK]
            d = jnp.zeros((block, kv_local), jnp.float32)
            for l in range(per_owner):
                r = jnp.dot(mj, up[l, j], preferred_element_type=jnp.float32)
                d = jnp.where(owner_of == l, r, d)
            ret_out[step, :, j * kv_local : (j + 1) * kv_local] = d.astype(jnp.bfloat16)
        if step:
            ret_copies[step] = remote(
                ret_out.at[step], ret_in.at[step], ret_ss.at[step], ret_rs.at[step],
                "store", (me_s + stores - step) % stores,
            )
            ret_copies[step].start()

    steps = [0] + order
    for place, step in enumerate(steps):
        lower(step)
        if place:
            raise_back(steps[place - 1])
    raise_back(steps[-1])

    for m in range(tensors - 1):
        base_copies[m].wait_recv()
        sq_copies[m].wait_recv()

    def give(step, src):
        def part(i, _):
            at = pl.ds(pl.multiple_of(i * mt, mt), mt)
            places = lax.broadcasted_iota(jnp.int32, (mt, block), 1) + step * block
            choose = jnp.where(places == tcol[at, :], 1.0, 0.0).astype(jnp.bfloat16)
            acc[at, :] = acc[at, :] + jnp.dot(choose, src[...], preferred_element_type=jnp.float32)
            return 0

        lax.fori_loop(0, rows // mt, part, 0)

    for step in steps:
        if step:
            ret_copies[step].wait_recv()
            give(step, ret_in.at[step])
        else:
            give(step, ret_out.at[step])

    def finish(i, _):
        at = pl.ds(pl.multiple_of(i * tile, tile), tile)
        square = sq_out[at, :]
        total = acc[at, :]
        for m in range(tensors - 1):
            square = square + sq_in[m, at, :]
            total = total + base_in[m, at, :].astype(jnp.float32)
        mean = jnp.sum(square, axis=1, keepdims=True) / (width * tensors)
        total = total * lax.rsqrt(mean + epsilon)
        c = cos_t[at, :]
        s = sin_t[at, :]
        for head in range(kv_local // HEAD):
            x = total[:, head * HEAD : (head + 1) * HEAD]
            y = x * c + pltpu.roll(x, HEAD // 2, 1) * s
            keys_o[at, head * HEAD : (head + 1) * HEAD] = y.astype(jnp.bfloat16)
        vals_o[at, :] = total[:, kv_local:].astype(jnp.bfloat16)
        return 0

    lax.fori_loop(0, rows // tile, finish, 0)

    for copy in sq_copies + base_copies:
        copy.wait_send()
    for copies in (tok_copies, low_copies, ret_copies):
        for copy in copies.values():
            copy.wait_send()


def fused(
    tokens,
    norm_gain,
    kv_weight,
    adapter_down,
    adapter_up,
    token_adapters,
    adapter_slot,
    request_lengths,
):
    rows, width = tokens.shape
    adapter_total = adapter_slot.shape[0]
    capacity = max(2, 5 * rows // (4 * adapter_total))
    stores = lax.axis_size("store")
    tensors = lax.axis_size("tensor")
    per_owner, _, _, kv_local = adapter_up.shape
    block = per_owner * capacity
    me = lax.axis_index("store")
    targets = place_rows(token_adapters[:, 0], adapter_slot, capacity)
    targets = (targets // block + stores - me) % stores * block + targets % block
    positions = positions_of(me * rows, rows, request_lengths)
    half = HEAD // 2
    frequency = jnp.exp(
        jnp.arange(half, dtype=jnp.float32) * (-2.0 * math.log(rope_theta) / HEAD)
    )
    angles = positions.astype(jnp.float32)[:, None] * frequency[None, :]
    cos_part = jnp.cos(angles)
    sin_part = jnp.sin(angles)
    cos_t = jnp.concatenate([cos_part, cos_part], axis=1)
    sin_t = jnp.concatenate([-sin_part, sin_part], axis=1)
    ranks = adapter_down.shape[2]
    vmem = pl.BlockSpec(memory_space=pltpu.VMEM)
    hbm = pl.BlockSpec(memory_space=pl.ANY)
    f32, bf16 = jnp.float32, jnp.bfloat16
    dma = pltpu.SemaphoreType.DMA
    return pl.pallas_call(
        functools.partial(fused_kernel, stores, tensors),
        out_shape=[jax.ShapeDtypeStruct((rows, kv_local), bf16)] * 2,
        in_specs=[vmem] * 7 + [hbm] * 2,
        out_specs=[vmem] * 2,
        scratch_shapes=[
            pltpu.VMEM((rows, width), bf16),
            pltpu.VMEM((width, 2 * kv_local * tensors), bf16),
            pltpu.VMEM((per_owner, width, ranks), bf16),
            pltpu.VMEM((rows, 128), f32),
            pltpu.VMEM((tensors - 1, rows, 128), f32),
            pltpu.VMEM((stores - 1, block, width), bf16),
            pltpu.VMEM((stores, block, width), bf16),
            pltpu.VMEM((rows, 2 * kv_local), f32),
            pltpu.VMEM((tensors - 1, rows, 2 * kv_local), bf16),
            pltpu.VMEM((tensors - 1, rows, 2 * kv_local), bf16),
            pltpu.VMEM((stores, block, ranks), f32),
            pltpu.VMEM((tensors - 1, stores, block, ranks), f32),
            pltpu.VMEM((stores, block, 2 * kv_local), bf16),
            pltpu.VMEM((stores, block, 2 * kv_local), bf16),
            dma((2,)),
            dma((tensors - 1,)),
            dma((tensors - 1,)),
            dma((stores,)),
            dma((stores,)),
            dma((tensors - 1,)),
            dma((tensors - 1,)),
            dma((stores, tensors - 1)),
            dma((stores, tensors - 1)),
            dma((stores,)),
            dma((stores,)),
        ],
        compiler_params=pltpu.CompilerParams(
            collective_id=0, has_side_effects=True, vmem_limit_bytes=60 * 1024 * 1024
        ),
    )(
        tokens,
        norm_gain[None, :],
        targets[None, :],
        targets[:, None],
        cos_t,
        sin_t,
        adapter_up,
        kv_weight.reshape(width, -1),
        adapter_down,
    )


def local(
    tokens,
    norm_gain,
    kv_weight,
    adapter_down,
    adapter_up,
    token_adapters,
    adapter_slot,
    request_lengths,
):
    row_count = tokens.shape[0]
    local_width = tokens.shape[1]
    adapter_total = adapter_slot.shape[0]
    capacity = max(2, 5 * row_count // (4 * adapter_total))
    store_size = lax.axis_size("store")
    per_owner = adapter_down.shape[0]
    kv_local = adapter_up.shape[3]
    widened = tokens.astype(jnp.float32)
    squares = lax.psum(jnp.sum(widened * widened, axis=1), "tensor")
    normed = (widened * lax.rsqrt(squares / D + epsilon)[:, None] * norm_gain[None, :]).astype(
        jnp.bfloat16
    )
    targets = place_rows(token_adapters[:, 0], adapter_slot, capacity)
    send_rows = (
        jnp.zeros((adapter_total * capacity, local_width), jnp.bfloat16).at[targets].set(normed)
    )
    send_rows = send_rows.reshape(store_size, per_owner, capacity, local_width)
    down_projected = jnp.einsum(
        "slcd,ldr->slcr",
        lax.all_to_all(send_rows, "store", split_axis=0, concat_axis=0, tiled=True),
        adapter_down,
        preferred_element_type=jnp.float32,
    )
    rank_total_sum = lax.psum(down_projected, "tensor")
    rank_activation = (rank_total_sum * adapter_scale).astype(jnp.bfloat16)
    split_rank = rank_activation.reshape(rank_activation.shape[:3] + (2, ADAPTER_RANK))
    update_rows = jnp.einsum(
        "slcjr,ljrk->slcjk", split_rank, adapter_up, preferred_element_type=jnp.float32
    )
    back_rows = update_rows.astype(jnp.bfloat16).reshape(
        rank_activation.shape[:3] + (2 * kv_local,)
    )
    returned = lax.all_to_all(back_rows, "store", split_axis=0, concat_axis=0, tiled=True)
    delta_rows = returned.reshape(adapter_total * capacity, 2, kv_local)[targets]
    partial_value = jnp.einsum("td,djk->tjk", normed, kv_weight, preferred_element_type=jnp.float32)
    base_part = lax.psum_scatter(partial_value, "tensor", scatter_dimension=2, tiled=True)
    combined = base_part + delta_rows.astype(jnp.float32)
    positions = positions_of(lax.axis_index("store") * row_count, row_count, request_lengths)
    new_keys = rotate(combined[:, 0, :], positions).astype(jnp.bfloat16)
    new_values = combined[:, 1, :].astype(jnp.bfloat16)
    return (new_keys, new_values)


def solution(mesh):
    small = mesh.shape["store"] <= 8 and mesh.shape["tensor"] > 1
    return jax.shard_map(
        fused if small else local,
        mesh=mesh,
        in_specs=(
            P("store", "tensor"),
            P("tensor"),
            P("tensor", None, None),
            P("store", "tensor", None),
            P("store", None, None, "tensor"),
            P("store", None),
            P(),
            P(),
        ),
        out_specs=(P("store", "tensor"), P("store", "tensor")),
        check_vma=False,
    )
```

```python
import functools
import math

import jax
import jax.numpy as jnp
from jax import lax
from jax.experimental import pallas as pl
from jax.experimental.pallas import tpu as pltpu
from jax.sharding import PartitionSpec as P

D = 8192
HEAD = 128
ADAPTER_RANK = 64


epsilon = 1e-05
adapter_scale = 2.0
rope_theta = 500000.0


def place_rows(adapter_ids, adapter_slot, capacity):
    catalog = jnp.arange(adapter_slot.shape[0], dtype=jnp.int32)
    slot_rows = jnp.sum(
        jnp.where(adapter_ids[:, None] == catalog[None, :], adapter_slot[None, :], 0), axis=1
    )
    row_order = jnp.arange(adapter_ids.shape[0], dtype=jnp.int32)
    same_earlier = (adapter_ids[:, None] == adapter_ids[None, :]) & (
        row_order[None, :] < row_order[:, None]
    )
    rank_rows = jnp.sum(same_earlier.astype(jnp.int32), axis=1)
    return slot_rows * capacity + rank_rows


def positions_of(first_row, row_count, lengths):
    global_rows = first_row + jnp.arange(row_count, dtype=jnp.int32)
    request_ends = jnp.cumsum(lengths)
    preceding = jnp.sum(
        jnp.where(request_ends[None, :] <= global_rows[:, None], lengths[None, :], 0), axis=1
    )
    return global_rows - preceding


def rotate(states, positions):
    per_head = states.reshape(states.shape[0], -1, HEAD)
    half_size = HEAD // 2
    frequency = jnp.exp(
        jnp.arange(half_size, dtype=jnp.float32) * (-2.0 * math.log(rope_theta) / HEAD)
    )
    angles = positions.astype(jnp.float32)[:, None] * frequency[None, :]
    cos_part = jnp.concatenate([jnp.cos(angles), jnp.cos(angles)], axis=1)[:, None, :]
    sin_part = jnp.concatenate([jnp.sin(angles), jnp.sin(angles)], axis=1)[:, None, :]
    low_half = per_head[..., :half_size]
    high_half = per_head[..., half_size:]
    turned = jnp.concatenate([-high_half, low_half], axis=-1)
    return (per_head * cos_part + turned * sin_part).reshape(states.shape)


MESH = pl.DeviceIdType.MESH


def send_order(size):
    return sorted(range(1, size), key=lambda step: (abs(2 * step - size), step))


def fused_kernel(
    stores,
    tensors,
    tok,
    gain,
    ids,
    slots,
    lengths,
    up,
    w_hbm,
    down_hbm,
    out,
    trow,
    tcol,
    cos_t,
    sin_t,
    g,
    w3,
    w,
    down,
    sq_out,
    sq_in,
    snd,
    rcv,
    acc,
    base_out,
    base_in,
    low_out,
    low_in,
    ret_out,
    ret_in,
    load_sem,
    sq_ss,
    sq_rs,
    tok_ss,
    tok_rs,
    base_ss,
    base_rs,
    low_ss,
    low_rs,
    ret_ss,
    ret_rs,
):
    rows, width = tok.shape
    per_owner = down.shape[0]
    block = rcv.shape[1]
    capacity = block // per_owner
    kv_local = up.shape[3]
    kv_whole = kv_local * tensors
    me_s = lax.axis_index("store")
    me_t = lax.axis_index("tensor")

    load_w = pltpu.make_async_copy(w_hbm, w3, load_sem.at[0])
    load_d = pltpu.make_async_copy(down_hbm, down, load_sem.at[1])
    load_w.start()
    load_d.start()

    barrier = pltpu.get_barrier_semaphore()
    for step in range(1, stores):
        pl.semaphore_signal(
            barrier, inc=1, device_id={"store": (me_s + step) % stores}, device_id_type=MESH
        )
    for step in range(1, tensors):
        pl.semaphore_signal(
            barrier, inc=1, device_id={"tensor": (me_t + step) % tensors}, device_id_type=MESH
        )
    pl.semaphore_wait(barrier, stores + tensors - 2)

    def remote(src, dst, ss, rs, axis, target):
        return pltpu.make_async_remote_copy(
            src_ref=src, dst_ref=dst, send_sem=ss, recv_sem=rs,
            device_id={axis: target}, device_id_type=MESH,
        )

    def to_tensor(step):
        return (me_t + step) % tensors

    tile = 128

    def scale(i, _):
        at = pl.ds(pl.multiple_of(i * tile, tile), tile)
        x = tok[at, :].astype(jnp.float32)
        g[at, :] = (x * gain[...]).astype(jnp.bfloat16)
        total = x[:, 0:128] * x[:, 0:128]
        for lane in range(1, width // 128):
            part = x[:, lane * 128 : (lane + 1) * 128]
            total = total + part * part
        sq_out[at, :] = total
        return 0

    lax.fori_loop(0, rows // tile, scale, 0)

    adapters = slots.shape[0]
    named = jnp.where(
        lax.broadcasted_iota(jnp.int32, (adapters, rows), 0) == ids[...], 1.0, 0.0
    )
    earlier = jnp.where(
        lax.broadcasted_iota(jnp.int32, (rows, rows), 0)
        < lax.broadcasted_iota(jnp.int32, (rows, rows), 1),
        1.0,
        0.0,
    ).astype(jnp.bfloat16)
    counts = jnp.dot(named.astype(jnp.bfloat16), earlier, preferred_element_type=jnp.float32)
    rank = jnp.sum(named * counts, axis=0, keepdims=True).astype(jnp.int32)
    slot = jnp.zeros((1, rows), jnp.int32)
    for a in range(adapters):
        slot = jnp.where(ids[...] == a, slots[a], slot)
    owner = slot // per_owner - me_s
    owner = jnp.where(owner < 0, owner + stores, owner)
    trow[...] = owner * block + slot % per_owner * capacity + rank

    sq_copies = [
        remote(sq_out, sq_in.at[m - 1], sq_ss.at[m - 1], sq_rs.at[m - 1], "tensor", to_tensor(m))
        for m in range(1, tensors)
    ]

    chunk = 512
    order = send_order(stores)
    tok_copies = {
        step: remote(
            snd.at[step - 1], rcv.at[step], tok_ss.at[step], tok_rs.at[step],
            "store", (me_s + step) % stores,
        )
        for step in order
    }

    def pick(step, dst):
        places = lax.broadcasted_iota(jnp.int32, (block, rows), 0) + step * block
        choose = jnp.where(places == trow[...], 1.0, 0.0).astype(jnp.bfloat16)

        def part(i, _):
            at = pl.ds(pl.multiple_of(i * chunk, chunk), chunk)
            dst[:, at] = jnp.dot(
                choose, g[:, at], preferred_element_type=jnp.float32
            ).astype(jnp.bfloat16)
            return 0

        lax.fori_loop(0, width // chunk, part, 0)

    for place, step in enumerate(order):
        pick(step, snd.at[step - 1])
        if place:
            tok_copies[order[place - 1]].start()
    pick(0, rcv.at[0])
    tok_copies[order[-1]].start()
    for copy in sq_copies:
        copy.start()

    load_w.wait()
    dt = 128
    two = lax.broadcasted_iota(jnp.int32, (dt, 2 * dt), 1) - 2 * lax.broadcasted_iota(
        jnp.int32, (dt, 2 * dt), 0
    )
    every = [jnp.where(two == j, 1.0, 0.0).astype(jnp.bfloat16) for j in range(2)]

    def part_kinds(i, _):
        at = pl.ds(pl.multiple_of(i * dt, dt), dt)
        x = w3[at].reshape(2 * dt, kv_whole)
        for j in range(2):
            w[at, j * kv_whole : (j + 1) * kv_whole] = jnp.dot(
                every[j], x, preferred_element_type=jnp.float32
            ).astype(jnp.bfloat16)
        return 0

    lax.fori_loop(0, width // dt, part_kinds, 0)
    base_copies = [
        remote(
            base_out.at[m - 1], base_in.at[m - 1], base_ss.at[m - 1], base_rs.at[m - 1],
            "tensor", to_tensor(m),
        )
        for m in range(1, tensors)
    ]
    mt = 256
    for m in list(range(1, tensors)) + [0]:
        for j in range(2):
            cols = pl.ds(
                pl.multiple_of(j * kv_whole + to_tensor(m) * kv_local, kv_local), kv_local
            )

            def base(i, _, m=m, j=j, cols=cols):
                at = pl.ds(pl.multiple_of(i * mt, mt), mt)
                r = jnp.dot(g[at, :], w[:, cols], preferred_element_type=jnp.float32)
                if m:
                    base_out[m - 1, at, j * kv_local : (j + 1) * kv_local] = r.astype(jnp.bfloat16)
                else:
                    acc[at, j * kv_local : (j + 1) * kv_local] = r
                return 0

            lax.fori_loop(0, rows // mt, base, 0)
        if m > 1:
            base_copies[m - 2].start()
        if m == 0:
            base_copies[tensors - 2].start()

    half = HEAD // 2
    lane = lax.broadcasted_iota(jnp.int32, (1, HEAD), 1)
    frequency = jnp.exp(
        (lane % half).astype(jnp.float32) * (-2.0 * math.log(rope_theta) / HEAD)
    )
    sign = jnp.where(lane < half, -1.0, 1.0)

    def tables(i, _):
        at = pl.ds(pl.multiple_of(i * tile, tile), tile)
        row = lax.broadcasted_iota(jnp.int32, (tile, HEAD), 0) + (me_s * rows + i * tile)
        position = row
        end = 0
        for r in range(lengths.shape[0]):
            end = end + lengths[r]
            position = jnp.where(row >= end, row - end, position)
        angles = position.astype(jnp.float32) * frequency
        cos_t[at, :] = jnp.cos(angles)
        sin_t[at, :] = jnp.sin(angles) * sign
        tcol[at, :] = jnp.broadcast_to(trow[:, at], (tile, tile)).T
        return 0

    lax.fori_loop(0, rows // tile, tables, 0)

    load_d.wait()
    owner_of = lax.broadcasted_iota(jnp.int32, (block, 1), 0) // capacity
    low_copies = {}

    def lower(step):
        if step:
            tok_copies[step].wait_recv()
        x = rcv[step]
        low = jnp.zeros((block, 128), jnp.float32)
        for l in range(per_owner):
            r = jnp.dot(x, down[l], preferred_element_type=jnp.float32)
            low = jnp.where(owner_of == l, r, low)
        low_out[step] = low
        for m in range(1, tensors):
            low_copies[step, m] = remote(
                low_out.at[step], low_in.at[m - 1, step], low_ss.at[step, m - 1],
                low_rs.at[step, m - 1], "tensor", to_tensor(m),
            )
            low_copies[step, m].start()

    ret_copies = {}

    def raise_back(step):
        total = low_out[step]
        for m in range(1, tensors):
            low_copies[step, m].wait_recv()
            total = total + low_in[m - 1, step]
        middle = (total * adapter_scale).astype(jnp.bfloat16)
        for j in range(2):
            mj = middle[:, j * ADAPTER_RANK : (j + 1) * ADAPTER_RANK]
            d = jnp.zeros((block, kv_local), jnp.float32)
            for l in range(per_owner):
                r = jnp.dot(mj, up[l, j], preferred_element_type=jnp.float32)
                d = jnp.where(owner_of == l, r, d)
            ret_out[step, :, j * kv_local : (j + 1) * kv_local] = d.astype(jnp.bfloat16)
        if step:
            ret_copies[step] = remote(
                ret_out.at[step], ret_in.at[step], ret_ss.at[step], ret_rs.at[step],
                "store", (me_s + stores - step) % stores,
            )
            ret_copies[step].start()

    steps = [0] + order
    for place, step in enumerate(steps):
        lower(step)
        if place:
            raise_back(steps[place - 1])
    raise_back(steps[-1])

    for m in range(tensors - 1):
        base_copies[m].wait_recv()
        sq_copies[m].wait_recv()

    def give(step, src):
        def part(i, _):
            at = pl.ds(pl.multiple_of(i * mt, mt), mt)
            places = lax.broadcasted_iota(jnp.int32, (mt, block), 1) + step * block
            choose = jnp.where(places == tcol[at, 0:1], 1.0, 0.0).astype(jnp.bfloat16)
            acc[at, :] = acc[at, :] + jnp.dot(choose, src[...], preferred_element_type=jnp.float32)
            return 0

        lax.fori_loop(0, rows // mt, part, 0)

    for step in steps:
        if step:
            ret_copies[step].wait_recv()
            give(step, ret_in.at[step])
        else:
            give(step, ret_out.at[step])

    def finish(i, _):
        at = pl.ds(pl.multiple_of(i * tile, tile), tile)
        square = sq_out[at, :]
        total = acc[at, :]
        for m in range(tensors - 1):
            square = square + sq_in[m, at, :]
            total = total + base_in[m, at, :].astype(jnp.float32)
        mean = jnp.sum(square, axis=1, keepdims=True) / (width * tensors)
        total = total * lax.rsqrt(mean + epsilon)
        c = cos_t[at, :]
        s = sin_t[at, :]
        for head in range(kv_local // HEAD):
            x = total[:, head * HEAD : (head + 1) * HEAD]
            y = x * c + pltpu.roll(x, HEAD // 2, 1) * s
            out[at, head * HEAD : (head + 1) * HEAD] = y.astype(jnp.bfloat16)
        out[at, kv_local:] = total[:, kv_local:].astype(jnp.bfloat16)
        return 0

    lax.fori_loop(0, rows // tile, finish, 0)

    for copy in sq_copies + base_copies:
        copy.wait_send()
    for copies in (tok_copies, low_copies, ret_copies):
        for copy in copies.values():
            copy.wait_send()


def fused(
    tokens,
    norm_gain,
    kv_weight,
    adapter_down,
    adapter_up,
    token_adapters,
    adapter_slot,
    request_lengths,
):
    rows, width = tokens.shape
    capacity = max(2, 5 * rows // (4 * adapter_slot.shape[0]))
    stores = lax.axis_size("store")
    tensors = lax.axis_size("tensor")
    per_owner, _, _, kv_local = adapter_up.shape
    block = per_owner * capacity
    ranks = adapter_down.shape[2]
    vmem = pl.BlockSpec(memory_space=pltpu.VMEM)
    smem = pl.BlockSpec(memory_space=pltpu.SMEM)
    hbm = pl.BlockSpec(memory_space=pl.ANY)
    f32, bf16 = jnp.float32, jnp.bfloat16
    dma = pltpu.SemaphoreType.DMA
    both = pl.pallas_call(
        functools.partial(fused_kernel, stores, tensors),
        out_shape=jax.ShapeDtypeStruct((rows, 2 * kv_local), bf16),
        in_specs=[vmem] * 3 + [smem] * 2 + [vmem] + [hbm] * 2,
        out_specs=vmem,
        scratch_shapes=[
            pltpu.VMEM((1, rows), jnp.int32),
            pltpu.VMEM((rows, 128), jnp.int32),
            pltpu.VMEM((rows, HEAD), f32),
            pltpu.VMEM((rows, HEAD), f32),
            pltpu.VMEM((rows, width), bf16),
            pltpu.VMEM((width, 2, kv_local * tensors), bf16),
            pltpu.VMEM((width, 2 * kv_local * tensors), bf16),
            pltpu.VMEM((per_owner, width, ranks), bf16),
            pltpu.VMEM((rows, 128), f32),
            pltpu.VMEM((tensors - 1, rows, 128), f32),
            pltpu.VMEM((stores - 1, block, width), bf16),
            pltpu.VMEM((stores, block, width), bf16),
            pltpu.VMEM((rows, 2 * kv_local), f32),
            pltpu.VMEM((tensors - 1, rows, 2 * kv_local), bf16),
            pltpu.VMEM((tensors - 1, rows, 2 * kv_local), bf16),
            pltpu.VMEM((stores, block, ranks), f32),
            pltpu.VMEM((tensors - 1, stores, block, ranks), f32),
            pltpu.VMEM((stores, block, 2 * kv_local), bf16),
            pltpu.VMEM((stores, block, 2 * kv_local), bf16),
            dma((2,)),
            dma((tensors - 1,)),
            dma((tensors - 1,)),
            dma((stores,)),
            dma((stores,)),
            dma((tensors - 1,)),
            dma((tensors - 1,)),
            dma((stores, tensors - 1)),
            dma((stores, tensors - 1)),
            dma((stores,)),
            dma((stores,)),
        ],
        compiler_params=pltpu.CompilerParams(
            collective_id=0, has_side_effects=True, vmem_limit_bytes=60 * 1024 * 1024
        ),
    )(
        tokens,
        norm_gain[None, :],
        token_adapters.reshape(1, rows),
        adapter_slot,
        request_lengths,
        adapter_up,
        kv_weight,
        adapter_down,
    )
    return both[:, :kv_local], both[:, kv_local:]


def local(
    tokens,
    norm_gain,
    kv_weight,
    adapter_down,
    adapter_up,
    token_adapters,
    adapter_slot,
    request_lengths,
):
    row_count = tokens.shape[0]
    local_width = tokens.shape[1]
    adapter_total = adapter_slot.shape[0]
    capacity = max(2, 5 * row_count // (4 * adapter_total))
    store_size = lax.axis_size("store")
    per_owner = adapter_down.shape[0]
    kv_local = adapter_up.shape[3]
    widened = tokens.astype(jnp.float32)
    squares = lax.psum(jnp.sum(widened * widened, axis=1), "tensor")
    normed = (widened * lax.rsqrt(squares / D + epsilon)[:, None] * norm_gain[None, :]).astype(
        jnp.bfloat16
    )
    targets = place_rows(token_adapters[:, 0], adapter_slot, capacity)
    send_rows = (
        jnp.zeros((adapter_total * capacity, local_width), jnp.bfloat16).at[targets].set(normed)
    )
    send_rows = send_rows.reshape(store_size, per_owner, capacity, local_width)
    down_projected = jnp.einsum(
        "slcd,ldr->slcr",
        lax.all_to_all(send_rows, "store", split_axis=0, concat_axis=0, tiled=True),
        adapter_down,
        preferred_element_type=jnp.float32,
    )
    rank_total_sum = lax.psum(down_projected, "tensor")
    rank_activation = (rank_total_sum * adapter_scale).astype(jnp.bfloat16)
    split_rank = rank_activation.reshape(rank_activation.shape[:3] + (2, ADAPTER_RANK))
    update_rows = jnp.einsum(
        "slcjr,ljrk->slcjk", split_rank, adapter_up, preferred_element_type=jnp.float32
    )
    back_rows = update_rows.astype(jnp.bfloat16).reshape(
        rank_activation.shape[:3] + (2 * kv_local,)
    )
    returned = lax.all_to_all(back_rows, "store", split_axis=0, concat_axis=0, tiled=True)
    delta_rows = returned.reshape(adapter_total * capacity, 2, kv_local)[targets]
    partial_value = jnp.einsum("td,djk->tjk", normed, kv_weight, preferred_element_type=jnp.float32)
    base_part = lax.psum_scatter(partial_value, "tensor", scatter_dimension=2, tiled=True)
    combined = base_part + delta_rows.astype(jnp.float32)
    positions = positions_of(lax.axis_index("store") * row_count, row_count, request_lengths)
    new_keys = rotate(combined[:, 0, :], positions).astype(jnp.bfloat16)
    new_values = combined[:, 1, :].astype(jnp.bfloat16)
    return (new_keys, new_values)


def solution(mesh):
    small = mesh.shape["store"] <= 8 and mesh.shape["tensor"] > 1
    return jax.shard_map(
        fused if small else local,
        mesh=mesh,
        in_specs=(
            P("store", "tensor"),
            P("tensor"),
            P("tensor", None, None),
            P("store", "tensor", None),
            P("store", None, None, "tensor"),
            P("store", None),
            P(),
            P(),
        ),
        out_specs=(P("store", "tensor"), P("store", "tensor")),
        check_vma=False,
    )
```

```python
import functools
import math

import jax
import jax.numpy as jnp
from jax import lax
from jax.experimental import pallas as pl
from jax.experimental.pallas import tpu as pltpu
from jax.sharding import PartitionSpec as P

D = 8192
HEAD = 128
ADAPTER_RANK = 64


epsilon = 1e-05
adapter_scale = 2.0
rope_theta = 500000.0


def place_rows(adapter_ids, adapter_slot, capacity):
    catalog = jnp.arange(adapter_slot.shape[0], dtype=jnp.int32)
    slot_rows = jnp.sum(
        jnp.where(adapter_ids[:, None] == catalog[None, :], adapter_slot[None, :], 0), axis=1
    )
    row_order = jnp.arange(adapter_ids.shape[0], dtype=jnp.int32)
    same_earlier = (adapter_ids[:, None] == adapter_ids[None, :]) & (
        row_order[None, :] < row_order[:, None]
    )
    rank_rows = jnp.sum(same_earlier.astype(jnp.int32), axis=1)
    return slot_rows * capacity + rank_rows


def positions_of(first_row, row_count, lengths):
    global_rows = first_row + jnp.arange(row_count, dtype=jnp.int32)
    request_ends = jnp.cumsum(lengths)
    preceding = jnp.sum(
        jnp.where(request_ends[None, :] <= global_rows[:, None], lengths[None, :], 0), axis=1
    )
    return global_rows - preceding


def rotate(states, positions):
    per_head = states.reshape(states.shape[0], -1, HEAD)
    half_size = HEAD // 2
    frequency = jnp.exp(
        jnp.arange(half_size, dtype=jnp.float32) * (-2.0 * math.log(rope_theta) / HEAD)
    )
    angles = positions.astype(jnp.float32)[:, None] * frequency[None, :]
    cos_part = jnp.concatenate([jnp.cos(angles), jnp.cos(angles)], axis=1)[:, None, :]
    sin_part = jnp.concatenate([jnp.sin(angles), jnp.sin(angles)], axis=1)[:, None, :]
    low_half = per_head[..., :half_size]
    high_half = per_head[..., half_size:]
    turned = jnp.concatenate([-high_half, low_half], axis=-1)
    return (per_head * cos_part + turned * sin_part).reshape(states.shape)


MESH = pl.DeviceIdType.MESH


def send_order(size):
    return sorted(range(1, size), key=lambda step: (abs(2 * step - size), step))


def fused_kernel(
    stores,
    tensors,
    tok,
    gain,
    ids,
    slots,
    lengths,
    up,
    w_hbm,
    down_hbm,
    out,
    trow,
    tcol,
    cos_t,
    sin_t,
    scale_t,
    g,
    w3,
    w,
    down,
    sq_out,
    sq_in,
    snd,
    rcv,
    acc,
    base_out,
    base_in,
    low_out,
    low_in,
    ret_out,
    ret_in,
    load_sem,
    sq_ss,
    sq_rs,
    tok_ss,
    tok_rs,
    base_ss,
    base_rs,
    low_ss,
    low_rs,
    ret_ss,
    ret_rs,
):
    rows, width = tok.shape
    per_owner = down.shape[0]
    block = rcv.shape[1]
    capacity = block // per_owner
    kv_local = up.shape[3]
    kv_whole = kv_local * tensors
    me_s = lax.axis_index("store")
    me_t = lax.axis_index("tensor")

    load_w = pltpu.make_async_copy(w_hbm, w3, load_sem.at[0])
    load_d = pltpu.make_async_copy(down_hbm, down, load_sem.at[1])
    load_w.start()
    load_d.start()

    barrier = pltpu.get_barrier_semaphore()
    for step in range(1, stores):
        pl.semaphore_signal(
            barrier, inc=1, device_id={"store": (me_s + step) % stores}, device_id_type=MESH
        )
    for step in range(1, tensors):
        pl.semaphore_signal(
            barrier, inc=1, device_id={"tensor": (me_t + step) % tensors}, device_id_type=MESH
        )
    pl.semaphore_wait(barrier, stores + tensors - 2)

    def remote(src, dst, ss, rs, axis, target):
        return pltpu.make_async_remote_copy(
            src_ref=src, dst_ref=dst, send_sem=ss, recv_sem=rs,
            device_id={axis: target}, device_id_type=MESH,
        )

    def to_tensor(step):
        return (me_t + step) % tensors

    tile = 128

    def scale(i, _):
        at = pl.ds(pl.multiple_of(i * tile, tile), tile)
        x = tok[at, :].astype(jnp.float32)
        g[at, :] = (x * gain[...]).astype(jnp.bfloat16)
        total = x[:, 0:128] * x[:, 0:128]
        for lane in range(1, width // 128):
            part = x[:, lane * 128 : (lane + 1) * 128]
            total = total + part * part
        sq_out[at, :] = total
        return 0

    lax.fori_loop(0, rows // tile, scale, 0)

    adapters = slots.shape[0]
    named = jnp.where(
        lax.broadcasted_iota(jnp.int32, (adapters, rows), 0) == ids[...], 1.0, 0.0
    )
    earlier = jnp.where(
        lax.broadcasted_iota(jnp.int32, (rows, rows), 0)
        < lax.broadcasted_iota(jnp.int32, (rows, rows), 1),
        1.0,
        0.0,
    ).astype(jnp.bfloat16)
    counts = jnp.dot(named.astype(jnp.bfloat16), earlier, preferred_element_type=jnp.float32)
    rank = jnp.sum(named * counts, axis=0, keepdims=True).astype(jnp.int32)
    slot = jnp.zeros((1, rows), jnp.int32)
    for a in range(adapters):
        slot = jnp.where(ids[...] == a, slots[a], slot)
    owner = slot // per_owner - me_s
    owner = jnp.where(owner < 0, owner + stores, owner)
    trow[...] = owner * block + slot % per_owner * capacity + rank

    sq_copies = [
        remote(sq_out, sq_in.at[m - 1], sq_ss.at[m - 1], sq_rs.at[m - 1], "tensor", to_tensor(m))
        for m in range(1, tensors)
    ]

    chunk = 512
    order = send_order(stores)
    tok_copies = {
        step: remote(
            snd.at[step - 1], rcv.at[step], tok_ss.at[step], tok_rs.at[step],
            "store", (me_s + step) % stores,
        )
        for step in order
    }

    def pick(step, dst):
        places = lax.broadcasted_iota(jnp.int32, (block, rows), 0) + step * block
        choose = jnp.where(places == trow[...], 1.0, 0.0).astype(jnp.bfloat16)

        def part(i, _):
            at = pl.ds(pl.multiple_of(i * chunk, chunk), chunk)
            dst[:, at] = jnp.dot(
                choose, g[:, at], preferred_element_type=jnp.float32
            ).astype(jnp.bfloat16)
            return 0

        lax.fori_loop(0, width // chunk, part, 0)

    for place, step in enumerate(order):
        pick(step, snd.at[step - 1])
        if place:
            tok_copies[order[place - 1]].start()
    pick(0, rcv.at[0])
    tok_copies[order[-1]].start()
    for copy in sq_copies:
        copy.start()

    load_w.wait()
    dt = 128
    two = lax.broadcasted_iota(jnp.int32, (dt, 2 * dt), 1) - 2 * lax.broadcasted_iota(
        jnp.int32, (dt, 2 * dt), 0
    )
    every = [jnp.where(two == j, 1.0, 0.0).astype(jnp.bfloat16) for j in range(2)]

    def part_kinds(i, _):
        at = pl.ds(pl.multiple_of(i * dt, dt), dt)
        x = w3[at].reshape(2 * dt, kv_whole)
        for j in range(2):
            w[at, j * kv_whole : (j + 1) * kv_whole] = jnp.dot(
                every[j], x, preferred_element_type=jnp.float32
            ).astype(jnp.bfloat16)
        return 0

    lax.fori_loop(0, width // dt, part_kinds, 0)
    base_copies = [
        remote(
            base_out.at[m - 1], base_in.at[m - 1], base_ss.at[m - 1], base_rs.at[m - 1],
            "tensor", to_tensor(m),
        )
        for m in range(1, tensors)
    ]
    mt = 256
    for m in list(range(1, tensors)) + [0]:
        for j in range(2):
            cols = pl.ds(
                pl.multiple_of(j * kv_whole + to_tensor(m) * kv_local, kv_local), kv_local
            )

            def base(i, _, m=m, j=j, cols=cols):
                at = pl.ds(pl.multiple_of(i * mt, mt), mt)
                r = jnp.dot(g[at, :], w[:, cols], preferred_element_type=jnp.float32)
                if m:
                    base_out[m - 1, at, j * kv_local : (j + 1) * kv_local] = r.astype(jnp.bfloat16)
                else:
                    acc[at, j * kv_local : (j + 1) * kv_local] = r
                return 0

            lax.fori_loop(0, rows // mt, base, 0)
        if m > 1:
            base_copies[m - 2].start()
        if m == 0:
            base_copies[tensors - 2].start()

    half = HEAD // 2
    lane = lax.broadcasted_iota(jnp.int32, (1, HEAD), 1)
    frequency = jnp.exp(
        (lane % half).astype(jnp.float32) * (-2.0 * math.log(rope_theta) / HEAD)
    )
    sign = jnp.where(lane < half, -1.0, 1.0)

    def tables(i, _):
        at = pl.ds(pl.multiple_of(i * tile, tile), tile)
        row = lax.broadcasted_iota(jnp.int32, (tile, HEAD), 0) + (me_s * rows + i * tile)
        position = row
        end = 0
        for r in range(lengths.shape[0]):
            end = end + lengths[r]
            position = jnp.where(row >= end, row - end, position)
        angles = position.astype(jnp.float32) * frequency
        cos_t[at, :] = jnp.cos(angles)
        sin_t[at, :] = jnp.sin(angles) * sign
        tcol[at, :] = jnp.broadcast_to(trow[:, at], (tile, tile)).T
        return 0

    lax.fori_loop(0, rows // tile, tables, 0)

    load_d.wait()
    owner_of = lax.broadcasted_iota(jnp.int32, (block, 1), 0) // capacity
    low_copies = {}

    def lower(step):
        if step:
            tok_copies[step].wait_recv()
        x = rcv[step]
        low = jnp.zeros((block, 128), jnp.float32)
        for l in range(per_owner):
            r = jnp.dot(x, down[l], preferred_element_type=jnp.float32)
            low = jnp.where(owner_of == l, r, low)
        low_out[step] = low
        for m in range(1, tensors):
            low_copies[step, m] = remote(
                low_out.at[step], low_in.at[m - 1, step], low_ss.at[step, m - 1],
                low_rs.at[step, m - 1], "tensor", to_tensor(m),
            )
            low_copies[step, m].start()

    ret_copies = {}

    def raise_back(step):
        total = low_out[step]
        for m in range(1, tensors):
            low_copies[step, m].wait_recv()
            total = total + low_in[m - 1, step]
        middle = (total * adapter_scale).astype(jnp.bfloat16)
        for j in range(2):
            mj = middle[:, j * ADAPTER_RANK : (j + 1) * ADAPTER_RANK]
            d = jnp.zeros((block, kv_local), jnp.float32)
            for l in range(per_owner):
                r = jnp.dot(mj, up[l, j], preferred_element_type=jnp.float32)
                d = jnp.where(owner_of == l, r, d)
            ret_out[step, :, j * kv_local : (j + 1) * kv_local] = d.astype(jnp.bfloat16)
        if step:
            ret_copies[step] = remote(
                ret_out.at[step], ret_in.at[step], ret_ss.at[step], ret_rs.at[step],
                "store", (me_s + stores - step) % stores,
            )
            ret_copies[step].start()

    def give(step, src):
        def part(i, _):
            at = pl.ds(pl.multiple_of(i * mt, mt), mt)
            places = lax.broadcasted_iota(jnp.int32, (mt, block), 1) + step * block
            choose = jnp.where(places == tcol[at, 0:1], 1.0, 0.0).astype(jnp.bfloat16)
            acc[at, :] = acc[at, :] + jnp.dot(choose, src[...], preferred_element_type=jnp.float32)
            return 0

        lax.fori_loop(0, rows // mt, part, 0)

    def settle(step):
        if step:
            ret_copies[step].wait_recv()
            give(step, ret_in.at[step])
        else:
            give(step, ret_out.at[step])

    def join(i, _):
        at = pl.ds(pl.multiple_of(i * tile, tile), tile)
        square = sq_out[at, :]
        total = acc[at, :]
        for m in range(tensors - 1):
            square = square + sq_in[m, at, :]
            total = total + base_in[m, at, :].astype(jnp.float32)
        mean = jnp.sum(square, axis=1, keepdims=True) / (width * tensors)
        scale_t[at, :] = jnp.broadcast_to(lax.rsqrt(mean + epsilon), (tile, 128))
        acc[at, :] = total
        return 0

    steps = [0] + order
    lag = 3
    for place, step in enumerate(steps):
        lower(step)
        if place:
            raise_back(steps[place - 1])
        if place >= lag:
            settle(steps[place - lag])
        if place == stores - 2:
            for m in range(tensors - 1):
                base_copies[m].wait_recv()
                sq_copies[m].wait_recv()
            lax.fori_loop(0, rows // tile, join, 0)
    raise_back(steps[-1])
    for step in steps[-lag:]:
        settle(step)

    def finish(i, _):
        at = pl.ds(pl.multiple_of(i * tile, tile), tile)
        total = acc[at, :] * scale_t[at, 0:1]
        c = cos_t[at, :]
        s = sin_t[at, :]
        for head in range(kv_local // HEAD):
            x = total[:, head * HEAD : (head + 1) * HEAD]
            y = x * c + pltpu.roll(x, HEAD // 2, 1) * s
            out[at, head * HEAD : (head + 1) * HEAD] = y.astype(jnp.bfloat16)
        out[at, kv_local:] = total[:, kv_local:].astype(jnp.bfloat16)
        return 0

    lax.fori_loop(0, rows // tile, finish, 0)

    for copy in sq_copies + base_copies:
        copy.wait_send()
    for copies in (tok_copies, low_copies, ret_copies):
        for copy in copies.values():
            copy.wait_send()


def fused(
    tokens,
    norm_gain,
    kv_weight,
    adapter_down,
    adapter_up,
    token_adapters,
    adapter_slot,
    request_lengths,
):
    rows, width = tokens.shape
    capacity = max(2, 5 * rows // (4 * adapter_slot.shape[0]))
    stores = lax.axis_size("store")
    tensors = lax.axis_size("tensor")
    per_owner, _, _, kv_local = adapter_up.shape
    block = per_owner * capacity
    ranks = adapter_down.shape[2]
    vmem = pl.BlockSpec(memory_space=pltpu.VMEM)
    smem = pl.BlockSpec(memory_space=pltpu.SMEM)
    hbm = pl.BlockSpec(memory_space=pl.ANY)
    f32, bf16 = jnp.float32, jnp.bfloat16
    dma = pltpu.SemaphoreType.DMA
    both = pl.pallas_call(
        functools.partial(fused_kernel, stores, tensors),
        out_shape=jax.ShapeDtypeStruct((rows, 2 * kv_local), bf16),
        in_specs=[vmem] * 3 + [smem] * 2 + [vmem] + [hbm] * 2,
        out_specs=vmem,
        scratch_shapes=[
            pltpu.VMEM((1, rows), jnp.int32),
            pltpu.VMEM((rows, 128), jnp.int32),
            pltpu.VMEM((rows, HEAD), f32),
            pltpu.VMEM((rows, HEAD), f32),
            pltpu.VMEM((rows, 128), f32),
            pltpu.VMEM((rows, width), bf16),
            pltpu.VMEM((width, 2, kv_local * tensors), bf16),
            pltpu.VMEM((width, 2 * kv_local * tensors), bf16),
            pltpu.VMEM((per_owner, width, ranks), bf16),
            pltpu.VMEM((rows, 128), f32),
            pltpu.VMEM((tensors - 1, rows, 128), f32),
            pltpu.VMEM((stores - 1, block, width), bf16),
            pltpu.VMEM((stores, block, width), bf16),
            pltpu.VMEM((rows, 2 * kv_local), f32),
            pltpu.VMEM((tensors - 1, rows, 2 * kv_local), bf16),
            pltpu.VMEM((tensors - 1, rows, 2 * kv_local), bf16),
            pltpu.VMEM((stores, block, ranks), f32),
            pltpu.VMEM((tensors - 1, stores, block, ranks), f32),
            pltpu.VMEM((stores, block, 2 * kv_local), bf16),
            pltpu.VMEM((stores, block, 2 * kv_local), bf16),
            dma((2,)),
            dma((tensors - 1,)),
            dma((tensors - 1,)),
            dma((stores,)),
            dma((stores,)),
            dma((tensors - 1,)),
            dma((tensors - 1,)),
            dma((stores, tensors - 1)),
            dma((stores, tensors - 1)),
            dma((stores,)),
            dma((stores,)),
        ],
        compiler_params=pltpu.CompilerParams(
            collective_id=0, has_side_effects=True, vmem_limit_bytes=60 * 1024 * 1024
        ),
    )(
        tokens,
        norm_gain[None, :],
        token_adapters.reshape(1, rows),
        adapter_slot,
        request_lengths,
        adapter_up,
        kv_weight,
        adapter_down,
    )
    return both[:, :kv_local], both[:, kv_local:]


def local(
    tokens,
    norm_gain,
    kv_weight,
    adapter_down,
    adapter_up,
    token_adapters,
    adapter_slot,
    request_lengths,
):
    row_count = tokens.shape[0]
    local_width = tokens.shape[1]
    adapter_total = adapter_slot.shape[0]
    capacity = max(2, 5 * row_count // (4 * adapter_total))
    store_size = lax.axis_size("store")
    per_owner = adapter_down.shape[0]
    kv_local = adapter_up.shape[3]
    widened = tokens.astype(jnp.float32)
    squares = lax.psum(jnp.sum(widened * widened, axis=1), "tensor")
    normed = (widened * lax.rsqrt(squares / D + epsilon)[:, None] * norm_gain[None, :]).astype(
        jnp.bfloat16
    )
    targets = place_rows(token_adapters[:, 0], adapter_slot, capacity)
    send_rows = (
        jnp.zeros((adapter_total * capacity, local_width), jnp.bfloat16).at[targets].set(normed)
    )
    send_rows = send_rows.reshape(store_size, per_owner, capacity, local_width)
    down_projected = jnp.einsum(
        "slcd,ldr->slcr",
        lax.all_to_all(send_rows, "store", split_axis=0, concat_axis=0, tiled=True),
        adapter_down,
        preferred_element_type=jnp.float32,
    )
    rank_total_sum = lax.psum(down_projected, "tensor")
    rank_activation = (rank_total_sum * adapter_scale).astype(jnp.bfloat16)
    split_rank = rank_activation.reshape(rank_activation.shape[:3] + (2, ADAPTER_RANK))
    update_rows = jnp.einsum(
        "slcjr,ljrk->slcjk", split_rank, adapter_up, preferred_element_type=jnp.float32
    )
    back_rows = update_rows.astype(jnp.bfloat16).reshape(
        rank_activation.shape[:3] + (2 * kv_local,)
    )
    returned = lax.all_to_all(back_rows, "store", split_axis=0, concat_axis=0, tiled=True)
    delta_rows = returned.reshape(adapter_total * capacity, 2, kv_local)[targets]
    partial_value = jnp.einsum("td,djk->tjk", normed, kv_weight, preferred_element_type=jnp.float32)
    base_part = lax.psum_scatter(partial_value, "tensor", scatter_dimension=2, tiled=True)
    combined = base_part + delta_rows.astype(jnp.float32)
    positions = positions_of(lax.axis_index("store") * row_count, row_count, request_lengths)
    new_keys = rotate(combined[:, 0, :], positions).astype(jnp.bfloat16)
    new_values = combined[:, 1, :].astype(jnp.bfloat16)
    return (new_keys, new_values)


def solution(mesh):
    small = mesh.shape["store"] <= 8 and mesh.shape["tensor"] > 1
    return jax.shard_map(
        fused if small else local,
        mesh=mesh,
        in_specs=(
            P("store", "tensor"),
            P("tensor"),
            P("tensor", None, None),
            P("store", "tensor", None),
            P("store", None, None, "tensor"),
            P("store", None),
            P(),
            P(),
        ),
        out_specs=(P("store", "tensor"), P("store", "tensor")),
        check_vma=False,
    )
```

```python
import functools
import math

import jax
import jax.numpy as jnp
from jax import lax
from jax.experimental import pallas as pl
from jax.experimental.pallas import tpu as pltpu
from jax.sharding import PartitionSpec as P

D = 8192
HEAD = 128
ADAPTER_RANK = 64


epsilon = 1e-05
adapter_scale = 2.0
rope_theta = 500000.0


def place_rows(adapter_ids, adapter_slot, capacity):
    catalog = jnp.arange(adapter_slot.shape[0], dtype=jnp.int32)
    slot_rows = jnp.sum(
        jnp.where(adapter_ids[:, None] == catalog[None, :], adapter_slot[None, :], 0), axis=1
    )
    row_order = jnp.arange(adapter_ids.shape[0], dtype=jnp.int32)
    same_earlier = (adapter_ids[:, None] == adapter_ids[None, :]) & (
        row_order[None, :] < row_order[:, None]
    )
    rank_rows = jnp.sum(same_earlier.astype(jnp.int32), axis=1)
    return slot_rows * capacity + rank_rows


def positions_of(first_row, row_count, lengths):
    global_rows = first_row + jnp.arange(row_count, dtype=jnp.int32)
    request_ends = jnp.cumsum(lengths)
    preceding = jnp.sum(
        jnp.where(request_ends[None, :] <= global_rows[:, None], lengths[None, :], 0), axis=1
    )
    return global_rows - preceding


def rotate(states, positions):
    per_head = states.reshape(states.shape[0], -1, HEAD)
    half_size = HEAD // 2
    frequency = jnp.exp(
        jnp.arange(half_size, dtype=jnp.float32) * (-2.0 * math.log(rope_theta) / HEAD)
    )
    angles = positions.astype(jnp.float32)[:, None] * frequency[None, :]
    cos_part = jnp.concatenate([jnp.cos(angles), jnp.cos(angles)], axis=1)[:, None, :]
    sin_part = jnp.concatenate([jnp.sin(angles), jnp.sin(angles)], axis=1)[:, None, :]
    low_half = per_head[..., :half_size]
    high_half = per_head[..., half_size:]
    turned = jnp.concatenate([-high_half, low_half], axis=-1)
    return (per_head * cos_part + turned * sin_part).reshape(states.shape)


MESH = pl.DeviceIdType.MESH


def send_order(size):
    return sorted(range(1, size), key=lambda step: (abs(2 * step - size), step))


def fused_kernel(
    stores,
    tensors,
    tok,
    gain,
    ids,
    slots,
    lengths,
    up,
    w_hbm,
    down_hbm,
    out,
    trow,
    tcol,
    cos_t,
    sin_t,
    scale_t,
    g,
    w3,
    w,
    down,
    sq_out,
    sq_in,
    snd,
    rcv,
    acc,
    base_out,
    base_in,
    low_out,
    low_in,
    ret_out,
    ret_in,
    load_sem,
    sq_ss,
    sq_rs,
    tok_ss,
    tok_rs,
    base_ss,
    base_rs,
    low_ss,
    low_rs,
    ret_ss,
    ret_rs,
):
    rows, width = tok.shape
    per_owner = down.shape[0]
    block = rcv.shape[1]
    capacity = block // per_owner
    kv_local = up.shape[3]
    kv_whole = kv_local * tensors
    me_s = lax.axis_index("store")
    me_t = lax.axis_index("tensor")

    load_w = pltpu.make_async_copy(w_hbm, w3, load_sem.at[0])
    load_d = pltpu.make_async_copy(down_hbm, down, load_sem.at[1])
    load_w.start()
    load_d.start()

    barrier = pltpu.get_barrier_semaphore()
    for step in range(1, stores):
        pl.semaphore_signal(
            barrier, inc=1, device_id={"store": (me_s + step) % stores}, device_id_type=MESH
        )
    for step in range(1, tensors):
        pl.semaphore_signal(
            barrier, inc=1, device_id={"tensor": (me_t + step) % tensors}, device_id_type=MESH
        )
    pl.semaphore_wait(barrier, stores + tensors - 2)

    def remote(src, dst, ss, rs, axis, target):
        return pltpu.make_async_remote_copy(
            src_ref=src, dst_ref=dst, send_sem=ss, recv_sem=rs,
            device_id={axis: target}, device_id_type=MESH,
        )

    def to_tensor(step):
        return (me_t + step) % tensors

    tile = 128

    def scale(i, _):
        at = pl.ds(pl.multiple_of(i * tile, tile), tile)
        x = tok[at, :].astype(jnp.float32)
        g[at, :] = (x * gain[...]).astype(jnp.bfloat16)
        total = x[:, 0:128] * x[:, 0:128]
        for lane in range(1, width // 128):
            part = x[:, lane * 128 : (lane + 1) * 128]
            total = total + part * part
        sq_out[at, :] = total
        return 0

    lax.fori_loop(0, rows // tile, scale, 0)

    adapters = slots.shape[0]
    named = jnp.where(
        lax.broadcasted_iota(jnp.int32, (adapters, rows), 0) == ids[...], 1.0, 0.0
    )
    earlier = jnp.where(
        lax.broadcasted_iota(jnp.int32, (rows, rows), 0)
        < lax.broadcasted_iota(jnp.int32, (rows, rows), 1),
        1.0,
        0.0,
    ).astype(jnp.bfloat16)
    counts = jnp.dot(named.astype(jnp.bfloat16), earlier, preferred_element_type=jnp.float32)
    rank = jnp.sum(named * counts, axis=0, keepdims=True).astype(jnp.int32)
    slot = jnp.zeros((1, rows), jnp.int32)
    for a in range(adapters):
        slot = jnp.where(ids[...] == a, slots[a], slot)
    owner = slot // per_owner - me_s
    owner = jnp.where(owner < 0, owner + stores, owner)
    trow[...] = owner * block + slot % per_owner * capacity + rank

    sq_copies = [
        remote(sq_out, sq_in.at[m - 1], sq_ss.at[m - 1], sq_rs.at[m - 1], "tensor", to_tensor(m))
        for m in range(1, tensors)
    ]

    chunk = 512
    order = send_order(stores)
    tok_copies = {
        step: remote(
            snd.at[step - 1], rcv.at[step], tok_ss.at[step], tok_rs.at[step],
            "store", (me_s + step) % stores,
        )
        for step in order
    }

    def pick(step, dst):
        places = lax.broadcasted_iota(jnp.int32, (block, rows), 0) + step * block
        choose = jnp.where(places == trow[...], 1.0, 0.0).astype(jnp.bfloat16)

        def part(i, _):
            at = pl.ds(pl.multiple_of(i * chunk, chunk), chunk)
            dst[:, at] = jnp.dot(
                choose, g[:, at], preferred_element_type=jnp.float32
            ).astype(jnp.bfloat16)
            return 0

        lax.fori_loop(0, width // chunk, part, 0)

    for place, step in enumerate(order):
        pick(step, snd.at[step - 1])
        if place:
            tok_copies[order[place - 1]].start()
    pick(0, rcv.at[0])
    tok_copies[order[-1]].start()
    for copy in sq_copies:
        copy.start()

    load_w.wait()
    dt = 128
    two = lax.broadcasted_iota(jnp.int32, (dt, 2 * dt), 1) - 2 * lax.broadcasted_iota(
        jnp.int32, (dt, 2 * dt), 0
    )
    every = [jnp.where(two == j, 1.0, 0.0).astype(jnp.bfloat16) for j in range(2)]

    def part_kinds(i, _):
        at = pl.ds(pl.multiple_of(i * dt, dt), dt)
        x = w3[at].reshape(2 * dt, kv_whole)
        for j in range(2):
            w[at, j * kv_whole : (j + 1) * kv_whole] = jnp.dot(
                every[j], x, preferred_element_type=jnp.float32
            ).astype(jnp.bfloat16)
        return 0

    lax.fori_loop(0, width // dt, part_kinds, 0)
    base_copies = [
        remote(
            base_out.at[m - 1], base_in.at[m - 1], base_ss.at[m - 1], base_rs.at[m - 1],
            "tensor", to_tensor(m),
        )
        for m in range(1, tensors)
    ]
    mt = 256
    for m in list(range(1, tensors)) + [0]:
        for j in range(2):
            cols = pl.ds(
                pl.multiple_of(j * kv_whole + to_tensor(m) * kv_local, kv_local), kv_local
            )

            def base(i, _, m=m, j=j, cols=cols):
                at = pl.ds(pl.multiple_of(i * mt, mt), mt)
                r = jnp.dot(g[at, :], w[:, cols], preferred_element_type=jnp.float32)
                if m:
                    base_out[m - 1, at, j * kv_local : (j + 1) * kv_local] = r.astype(jnp.bfloat16)
                else:
                    acc[at, j * kv_local : (j + 1) * kv_local] = r
                return 0

            lax.fori_loop(0, rows // mt, base, 0)
        if m > 1:
            base_copies[m - 2].start()
        if m == 0:
            base_copies[tensors - 2].start()

    half = HEAD // 2
    lane = lax.broadcasted_iota(jnp.int32, (1, HEAD), 1)
    frequency = jnp.exp(
        (lane % half).astype(jnp.float32) * (-2.0 * math.log(rope_theta) / HEAD)
    )
    sign = jnp.where(lane < half, -1.0, 1.0)

    def tables(i, _):
        at = pl.ds(pl.multiple_of(i * tile, tile), tile)
        row = lax.broadcasted_iota(jnp.int32, (tile, HEAD), 0) + (me_s * rows + i * tile)
        position = row
        end = 0
        for r in range(lengths.shape[0]):
            end = end + lengths[r]
            position = jnp.where(row >= end, row - end, position)
        angles = position.astype(jnp.float32) * frequency
        cos_t[at, :] = jnp.cos(angles)
        sin_t[at, :] = jnp.sin(angles) * sign
        tcol[at, :] = jnp.broadcast_to(trow[:, at], (tile, tile)).T
        return 0

    lax.fori_loop(0, rows // tile, tables, 0)

    load_d.wait()
    owner_of = lax.broadcasted_iota(jnp.int32, (block, 1), 0) // capacity
    low_copies = {}

    def lower(step):
        if step:
            tok_copies[step].wait_recv()
        x = rcv[step]
        low = jnp.zeros((block, 128), jnp.float32)
        for l in range(per_owner):
            r = jnp.dot(x, down[l], preferred_element_type=jnp.float32)
            low = jnp.where(owner_of == l, r, low)
        low_out[step] = low
        for m in range(1, tensors):
            low_copies[step, m] = remote(
                low_out.at[step], low_in.at[m - 1, step], low_ss.at[step, m - 1],
                low_rs.at[step, m - 1], "tensor", to_tensor(m),
            )
            low_copies[step, m].start()

    ret_copies = {}

    def raise_back(step):
        total = low_out[step]
        for m in range(1, tensors):
            low_copies[step, m].wait_recv()
            total = total + low_in[m - 1, step]
        middle = (total * adapter_scale).astype(jnp.bfloat16)
        for j in range(2):
            mj = middle[:, j * ADAPTER_RANK : (j + 1) * ADAPTER_RANK]
            d = jnp.zeros((block, kv_local), jnp.float32)
            for l in range(per_owner):
                r = jnp.dot(mj, up[l, j], preferred_element_type=jnp.float32)
                d = jnp.where(owner_of == l, r, d)
            ret_out[step, :, j * kv_local : (j + 1) * kv_local] = d.astype(jnp.bfloat16)
        if step:
            ret_copies[step] = remote(
                ret_out.at[step], ret_in.at[step], ret_ss.at[step], ret_rs.at[step],
                "store", (me_s + stores - step) % stores,
            )
            ret_copies[step].start()

    def give(step, src):
        def part(i, _):
            at = pl.ds(pl.multiple_of(i * mt, mt), mt)
            places = lax.broadcasted_iota(jnp.int32, (mt, block), 1) + step * block
            choose = jnp.where(places == tcol[at, 0:1], 1.0, 0.0).astype(jnp.bfloat16)
            acc[at, :] = acc[at, :] + jnp.dot(choose, src[...], preferred_element_type=jnp.float32)
            return 0

        lax.fori_loop(0, rows // mt, part, 0)

    def settle(step):
        if step:
            ret_copies[step].wait_recv()
            give(step, ret_in.at[step])
        else:
            give(step, ret_out.at[step])

    def join(i, _):
        at = pl.ds(pl.multiple_of(i * tile, tile), tile)
        square = sq_out[at, :]
        total = acc[at, :]
        for m in range(tensors - 1):
            square = square + sq_in[m, at, :]
            total = total + base_in[m, at, :].astype(jnp.float32)
        mean = jnp.sum(square, axis=1, keepdims=True) / (width * tensors)
        scale_t[at, :] = jnp.broadcast_to(lax.rsqrt(mean + epsilon), (tile, 128))
        acc[at, :] = total
        return 0

    steps = [0] + order
    for place, step in enumerate(steps):
        lower(step)
        if place:
            raise_back(steps[place - 1])
        if place == stores - 2:
            for m in range(tensors - 1):
                base_copies[m].wait_recv()
                sq_copies[m].wait_recv()
            lax.fori_loop(0, rows // tile, join, 0)
    raise_back(steps[-1])
    for step in steps:
        settle(step)

    def finish(i, _):
        at = pl.ds(pl.multiple_of(i * tile, tile), tile)
        total = acc[at, :] * scale_t[at, 0:1]
        c = cos_t[at, :]
        s = sin_t[at, :]
        for head in range(kv_local // HEAD):
            x = total[:, head * HEAD : (head + 1) * HEAD]
            y = x * c + pltpu.roll(x, HEAD // 2, 1) * s
            out[at, head * HEAD : (head + 1) * HEAD] = y.astype(jnp.bfloat16)
        out[at, kv_local:] = total[:, kv_local:].astype(jnp.bfloat16)
        return 0

    lax.fori_loop(0, rows // tile, finish, 0)

    for copy in sq_copies + base_copies:
        copy.wait_send()
    for copies in (tok_copies, low_copies, ret_copies):
        for copy in copies.values():
            copy.wait_send()


def fused(
    tokens,
    norm_gain,
    kv_weight,
    adapter_down,
    adapter_up,
    token_adapters,
    adapter_slot,
    request_lengths,
):
    rows, width = tokens.shape
    capacity = max(2, 5 * rows // (4 * adapter_slot.shape[0]))
    stores = lax.axis_size("store")
    tensors = lax.axis_size("tensor")
    per_owner, _, _, kv_local = adapter_up.shape
    block = per_owner * capacity
    ranks = adapter_down.shape[2]
    vmem = pl.BlockSpec(memory_space=pltpu.VMEM)
    smem = pl.BlockSpec(memory_space=pltpu.SMEM)
    hbm = pl.BlockSpec(memory_space=pl.ANY)
    f32, bf16 = jnp.float32, jnp.bfloat16
    dma = pltpu.SemaphoreType.DMA
    both = pl.pallas_call(
        functools.partial(fused_kernel, stores, tensors),
        out_shape=jax.ShapeDtypeStruct((rows, 2 * kv_local), bf16),
        in_specs=[vmem] * 3 + [smem] * 2 + [vmem] + [hbm] * 2,
        out_specs=vmem,
        scratch_shapes=[
            pltpu.VMEM((1, rows), jnp.int32),
            pltpu.VMEM((rows, 128), jnp.int32),
            pltpu.VMEM((rows, HEAD), f32),
            pltpu.VMEM((rows, HEAD), f32),
            pltpu.VMEM((rows, 128), f32),
            pltpu.VMEM((rows, width), bf16),
            pltpu.VMEM((width, 2, kv_local * tensors), bf16),
            pltpu.VMEM((width, 2 * kv_local * tensors), bf16),
            pltpu.VMEM((per_owner, width, ranks), bf16),
            pltpu.VMEM((rows, 128), f32),
            pltpu.VMEM((tensors - 1, rows, 128), f32),
            pltpu.VMEM((stores - 1, block, width), bf16),
            pltpu.VMEM((stores, block, width), bf16),
            pltpu.VMEM((rows, 2 * kv_local), f32),
            pltpu.VMEM((tensors - 1, rows, 2 * kv_local), bf16),
            pltpu.VMEM((tensors - 1, rows, 2 * kv_local), bf16),
            pltpu.VMEM((stores, block, ranks), f32),
            pltpu.VMEM((tensors - 1, stores, block, ranks), f32),
            pltpu.VMEM((stores, block, 2 * kv_local), bf16),
            pltpu.VMEM((stores, block, 2 * kv_local), bf16),
            dma((2,)),
            dma((tensors - 1,)),
            dma((tensors - 1,)),
            dma((stores,)),
            dma((stores,)),
            dma((tensors - 1,)),
            dma((tensors - 1,)),
            dma((stores, tensors - 1)),
            dma((stores, tensors - 1)),
            dma((stores,)),
            dma((stores,)),
        ],
        compiler_params=pltpu.CompilerParams(
            collective_id=0, has_side_effects=True, vmem_limit_bytes=60 * 1024 * 1024
        ),
    )(
        tokens,
        norm_gain[None, :],
        token_adapters.reshape(1, rows),
        adapter_slot,
        request_lengths,
        adapter_up,
        kv_weight,
        adapter_down,
    )
    return both[:, :kv_local], both[:, kv_local:]


def local(
    tokens,
    norm_gain,
    kv_weight,
    adapter_down,
    adapter_up,
    token_adapters,
    adapter_slot,
    request_lengths,
):
    row_count = tokens.shape[0]
    local_width = tokens.shape[1]
    adapter_total = adapter_slot.shape[0]
    capacity = max(2, 5 * row_count // (4 * adapter_total))
    store_size = lax.axis_size("store")
    per_owner = adapter_down.shape[0]
    kv_local = adapter_up.shape[3]
    widened = tokens.astype(jnp.float32)
    squares = lax.psum(jnp.sum(widened * widened, axis=1), "tensor")
    normed = (widened * lax.rsqrt(squares / D + epsilon)[:, None] * norm_gain[None, :]).astype(
        jnp.bfloat16
    )
    targets = place_rows(token_adapters[:, 0], adapter_slot, capacity)
    send_rows = (
        jnp.zeros((adapter_total * capacity, local_width), jnp.bfloat16).at[targets].set(normed)
    )
    send_rows = send_rows.reshape(store_size, per_owner, capacity, local_width)
    down_projected = jnp.einsum(
        "slcd,ldr->slcr",
        lax.all_to_all(send_rows, "store", split_axis=0, concat_axis=0, tiled=True),
        adapter_down,
        preferred_element_type=jnp.float32,
    )
    rank_total_sum = lax.psum(down_projected, "tensor")
    rank_activation = (rank_total_sum * adapter_scale).astype(jnp.bfloat16)
    split_rank = rank_activation.reshape(rank_activation.shape[:3] + (2, ADAPTER_RANK))
    update_rows = jnp.einsum(
        "slcjr,ljrk->slcjk", split_rank, adapter_up, preferred_element_type=jnp.float32
    )
    back_rows = update_rows.astype(jnp.bfloat16).reshape(
        rank_activation.shape[:3] + (2 * kv_local,)
    )
    returned = lax.all_to_all(back_rows, "store", split_axis=0, concat_axis=0, tiled=True)
    delta_rows = returned.reshape(adapter_total * capacity, 2, kv_local)[targets]
    partial_value = jnp.einsum("td,djk->tjk", normed, kv_weight, preferred_element_type=jnp.float32)
    base_part = lax.psum_scatter(partial_value, "tensor", scatter_dimension=2, tiled=True)
    combined = base_part + delta_rows.astype(jnp.float32)
    positions = positions_of(lax.axis_index("store") * row_count, row_count, request_lengths)
    new_keys = rotate(combined[:, 0, :], positions).astype(jnp.bfloat16)
    new_values = combined[:, 1, :].astype(jnp.bfloat16)
    return (new_keys, new_values)


def solution(mesh):
    small = mesh.shape["store"] <= 8 and mesh.shape["tensor"] > 1
    return jax.shard_map(
        fused if small else local,
        mesh=mesh,
        in_specs=(
            P("store", "tensor"),
            P("tensor"),
            P("tensor", None, None),
            P("store", "tensor", None),
            P("store", None, None, "tensor"),
            P("store", None),
            P(),
            P(),
        ),
        out_specs=(P("store", "tensor"), P("store", "tensor")),
        check_vma=False,
    )
```
